32 devices in a mesh: blk: 8 (over y, x, core), src: 4 (over z).
Axes of the slice: x: 2, y: 2, z: 4, core: 2. Of those that a mesh axis runs over, the one named last changes fastest.
Arguments:
- lower_blocks: float32 [2, 2048, 2, 2048], P(None, 'blk', None, 'src'), may hold values from -0.09375 to 0.09375
- inverse_blocks: float32 [2, 2048, 2, 2048], P(None, 'src', None, 'blk'), may hold values from -0.09375 to 0.09375
- source_terms: float32 [2, 2048, 2, 1536], P(None, 'blk', None, 'src'), may hold values from -6 to 6
- previous_panel: float32 [2048, 2, 1536], P('blk', None, 'src'), may hold values from -6 to 6
Outputs:
- solution: float32 [2, 2048, 2, 1536], P(None, 'blk', None, 'src')
The draws below stay inside these ranges and needn't reach their ends.
All inputs are finite; a program needn't handle non-finite values.
Results may differ from the reference program's by a relative error of at most 0.0001.
Values sent between devices are 32-bit elements; how exact they have to be, the bound alone decides.
No kernel may reach another device: no remote copies, remote signals or barrier semaphores. Data moves between devices by JAX's collectives and lax.ppermute only.
A program may use at most 128 MiB of HBM per device.

```python
import jax
import jax.numpy as jnp
from jax import lax

NB = 2048
STEPS = 2
SOURCES = 1536


def level_of(rng, shape, split, least, top_value):
    def one(axis_at, shards_of):
        steps = jax.random.uniform(jax.random.fold_in(jax.random.fold_in(rng, 6), axis_at), (shards_of,), jnp.float32, least / len(split), top_value / len(split))
        return jnp.repeat(jnp.exp(steps), shape[axis_at] // shards_of).reshape((-1,) + (1,) * (len(shape) - axis_at - 1))

    loudness = one(*split[0])
    for cut in split[1:]:
        loudness = loudness * one(*cut)
    return loudness


def centred(stream_key, extent, spread, bound, shards=(), held_as=jnp.bfloat16):
    factor_of = level_of(stream_key, extent, shards, -0.22, 0.18) if shards else 1.0
    values = jax.random.normal(stream_key, extent, jnp.float32) * spread * factor_of
    return jnp.minimum(jnp.maximum(values, -bound), bound).astype(held_as)


def setup_inputs(seed: int = 0) -> dict:
    key_of = jax.random.split(jax.random.key(seed), 5)
    return {
        "lower_blocks": centred(key_of[0], (STEPS, NB, 2, NB), (2 * NB) ** -0.5, 0.09375, ((1, 8), (3, 4)), jnp.float32),
        "inverse_blocks": centred(key_of[1], (STEPS, NB, 2, NB), (2 * NB) ** -0.5, 0.09375, ((1, 4), (3, 8)), jnp.float32),
        "source_terms": centred(key_of[2], (STEPS, NB, 2, SOURCES), 1.0, 6.0, ((1, 8), (3, 4)), jnp.float32),
        "previous_panel": centred(key_of[3], (NB, 2, SOURCES), 1.0, 6.0, ((0, 8), (2, 4)), jnp.float32),
    }


def complex_product(matrix, panel):
    high = lax.Precision.HIGHEST
    real_m = matrix[:, 0, :]
    imag_m = matrix[:, 1, :]
    real_x = panel[:, 0, :]
    imag_x = panel[:, 1, :]
    real_out = jnp.dot(real_m, real_x, precision=high, preferred_element_type=jnp.float32) - jnp.dot(imag_m, imag_x, precision=high, preferred_element_type=jnp.float32)
    imag_out = jnp.dot(real_m, imag_x, precision=high, preferred_element_type=jnp.float32) + jnp.dot(imag_m, real_x, precision=high, preferred_element_type=jnp.float32)
    return jnp.stack([real_out, imag_out], axis=1)


def reference(lower_blocks, inverse_blocks, source_terms, previous_panel):
    panel = previous_panel
    results = []
    for step in range(STEPS):
        carried = source_terms[step] - complex_product(lower_blocks[step], panel)
        panel = complex_product(inverse_blocks[step], carried)
        results.append(panel)
    return jnp.stack(results, axis=0)
```

```python
import jax
import jax.numpy as jnp
from jax import lax
from jax.sharding import PartitionSpec as P

STEPS = 2


def complex_product(matrix, panel):
    high = lax.Precision.HIGHEST
    real_m = matrix[:, 0, :]
    imag_m = matrix[:, 1, :]
    real_x = panel[:, 0, :]
    imag_x = panel[:, 1, :]
    real_out = jnp.dot(
        real_m, real_x, precision=high, preferred_element_type=jnp.float32
    ) - jnp.dot(imag_m, imag_x, precision=high, preferred_element_type=jnp.float32)
    imag_out = jnp.dot(
        real_m, imag_x, precision=high, preferred_element_type=jnp.float32
    ) + jnp.dot(imag_m, real_x, precision=high, preferred_element_type=jnp.float32)
    return jnp.stack([real_out, imag_out], axis=1)


def gathered(lower_blocks, inverse_blocks, source_terms, previous_panel):
    results = []
    panel = previous_panel
    for step in range(STEPS):
        lower_step = lax.all_gather(lower_blocks[step], "src", axis=2, tiled=True)
        inverse_step = lax.all_gather(inverse_blocks[step], "src", axis=0, tiled=True)
        whole = lax.all_gather(panel, "blk", axis=0, tiled=True)
        carried = source_terms[step] - complex_product(lower_step, whole)
        panel = lax.psum_scatter(
            complex_product(inverse_step, carried), "blk", scatter_dimension=0, tiled=True
        )
        results.append(panel)
    return jnp.stack(results, axis=0)


def move_src(value, pairs):
    return lax.ppermute(value, "src", pairs)


def swap_pair(value):
    return move_src(value, [(0, 1), (1, 0), (2, 3), (3, 2)])


def swap_bit(value, bit):
    return lax.ppermute(value, "blk", [(b, b ^ bit) for b in range(8)])


def over_core(value):
    return swap_bit(value, 1)


def over_x(value):
    return swap_bit(value, 2)


def over_y(value):
    return swap_bit(value, 4)


def far_block(own):
    near = move_src(own, [(1, 2), (2, 1)])
    outer = move_src(own, [(0, 1), (3, 2)])
    crossed = move_src(outer, [(1, 2), (2, 1)])
    relayed = move_src(near, [(1, 0), (2, 3)])
    return crossed + relayed


def flip_if(flag, value, axis):
    first, second = jnp.split(value, 2, axis=axis)
    return jnp.where(flag, jnp.concatenate([second, first], axis=axis), value)


def product(matrix, panel):
    return jnp.dot(
        matrix, panel, precision=lax.Precision.HIGH, preferred_element_type=jnp.float32
    )


def combine(both):
    real_m, imag_m = jnp.split(both, 2, axis=0)
    rr, ri = jnp.split(real_m, 2, axis=1)
    ir, ii = jnp.split(imag_m, 2, axis=1)
    return jnp.concatenate([rr - ii, ri + ir], axis=1)


def paired(lower_blocks, inverse_blocks, source_terms, previous_panel):
    b = lax.axis_index("blk")
    s = lax.axis_index("src")
    c, x, y = b % 2, (b // 2) % 2, b // 4
    own_x = x == s % 2
    own_y = y == s // 2
    rows = previous_panel.shape[0]
    cols = previous_panel.shape[2]
    piece = rows // 2

    def flat(value):
        return value.reshape(rows, 2 * cols)

    def lower_of(step):
        value = jnp.swapaxes(lower_blocks[step], 0, 1)
        deep = value.shape[2]
        value = value.reshape(2, rows, 2, 2, deep // 4)
        value = flip_if(c == 1, value, 2)
        value = flip_if(x == 1, value, 3)
        return value.reshape(2 * rows, deep)

    def inverse_of(step):
        value = jnp.swapaxes(inverse_blocks[step], 0, 1)
        tall = value.shape[1]
        value = value.reshape(2, 2, 2, tall // 4, rows)
        value = flip_if(c == 1, value, 1)
        value = flip_if(x == 1, value, 2)
        return value.reshape(2 * tall, rows)

    def gather(own, first, second):
        near = first(own)
        held = [own, near, second(own), second(near)]
        return held + [over_core(v) for v in held]

    def stacked(held, x_first):
        one, two = (1, 2) if x_first else (2, 1)
        upper = jnp.concatenate([held[0], held[one], held[4], held[4 + one]], axis=0)
        lower = jnp.concatenate(
            [held[two], held[3], held[4 + two], held[7]], axis=0
        )
        return jnp.where(own_y, upper, lower), jnp.where(own_y, lower, upper)

    def scatter(near_y, far_y, x_first):
        def cut(value):
            return value.reshape(2, 2, piece, 2 * cols)

        whole = jnp.stack([cut(near_y), cut(far_y)])
        half = whole[:, 0] + over_core(whole[:, 1])
        if x_first:
            quarter = half[:, 0] + over_x(half[:, 1])
            return quarter[0] + over_y(quarter[1])
        quarter = half[0] + over_y(half[1])
        return quarter[0] + over_x(quarter[1])

    lowers = []
    inverses = []
    for step in range(STEPS):
        own = lower_of(step)
        lowers.append((own, far_block(own)))
        own = inverse_of(step)
        inverses.append((own, far_block(own)))

    start = flat(previous_panel)
    top, bottom = start[:piece], start[piece:]
    mine = jnp.where(x == 0, top, bottom)
    other = over_x(jnp.where(x == 0, bottom, top))
    panel_a = jnp.where(own_x, mine, other)
    panel_b = swap_pair(jnp.where(own_x, other, mine))

    results = []
    for step in range(STEPS):
        low_own, low_far = lowers[step]
        inv_own, inv_far = inverses[step]
        near_a, far_a = stacked(gather(panel_a, over_x, over_y), True)
        near_b, far_b = stacked(gather(panel_b, over_y, over_x), False)
        sum_a = combine(product(low_own, near_a) + product(low_far, far_a))
        sum_b = combine(product(low_own, near_b) + product(low_far, far_b))
        part_a = flat(source_terms[step]) - sum_a
        part_b = -sum_b
        carried_a = part_a + swap_pair(part_b)
        carried_b = part_b + swap_pair(part_a)
        out = []
        for carried, x_first in ((carried_a, True), (carried_b, False)):
            own_rows = combine(product(inv_own, carried))
            far_rows = combine(product(inv_far, carried))
            near_y = jnp.where(own_y, own_rows, far_rows)
            far_y = jnp.where(own_y, far_rows, own_rows)
            out.append(scatter(near_y, far_y, x_first))
        panel_a, panel_b = out
        back = swap_pair(panel_b)
        mine = jnp.where(own_x, panel_a, back)
        other = over_x(jnp.where(own_x, back, panel_a))
        low_rows = jnp.where(x == 0, mine, other)
        high_rows = jnp.where(x == 0, other, mine)
        results.append(
            jnp.concatenate([low_rows, high_rows], axis=0).reshape(rows, 2, cols)
        )
    return jnp.stack(results, axis=0)


def solution(mesh):
    small = mesh.shape["blk"] == 8 and mesh.shape["src"] == 4
    return jax.shard_map(
        paired if small else gathered,
        mesh=mesh,
        in_specs=(
            P(None, "blk", None, "src"),
            P(None, "src", None, "blk"),
            P(None, "blk", None, "src"),
            P("blk", None, "src"),
        ),
        out_specs=P(None, "blk", None, "src"),
        check_vma=False,
    )
```
